32 devices in a mesh: dp: 32 (over z, y, x, core).
Axes of the slice: x: 2, y: 2, z: 4, core: 2. Of those that a mesh axis runs over, the one named last changes fastest.
Arguments:
- inputs: bfloat16 [128, 197, 768], P('dp'), may hold values from -6 to 6
- out_grad: bfloat16 [128, 197, 768], P('dp'), may hold values from -6 to 6
- w_qkv: float32 [768, 2304], P(None, 'dp'), may hold values from -5 to 5
- w_out: float32 [768, 768], P(None, 'dp'), may hold values from -0.625 to 0.625
- w_fc1: float32 [768, 3072], P(None, 'dp'), may hold values from -0.21875 to 0.21875
- w_fc2: float32 [768, 3072], P(None, 'dp'), may hold values from -0.109375 to 0.109375
- norm_params: float32 [4, 768], P(None, 'dp'), may hold values from -2 to 2
- mom_qkv: float32 [768, 2304], P(None, 'dp'), may hold values from -128 to 128
- mom_out: float32 [768, 768], P(None, 'dp'), may hold values from -128 to 128
- mom_fc1: float32 [768, 3072], P(None, 'dp'), may hold values from -128 to 128
- mom_fc2: float32 [768, 3072], P(None, 'dp'), may hold values from -128 to 128
- adam_mean: float32 [4, 768], P(None, 'dp'), may hold values from -64 to 64
- adam_var: float32 [4, 768], P(None, 'dp'), may hold values from 5 to 50
Outputs:
- block_out: bfloat16 [128, 197, 768], P('dp')
- input_grad: bfloat16 [128, 197, 768], P('dp')
- grad_qkv: float32 [768, 2304], P(None, 'dp')
- grad_out: float32 [768, 768], P(None, 'dp')
- grad_fc1: float32 [768, 3072], P(None, 'dp')
- grad_fc2: float32 [768, 3072], P(None, 'dp')
- grad_norms: float32 [4, 768], P(None, 'dp')
- new_qkv: float32 [768, 2304], P(None, 'dp')
- new_out: float32 [768, 768], P(None, 'dp')
- new_fc1: float32 [768, 3072], P(None, 'dp')
- new_fc2: float32 [768, 3072], P(None, 'dp')
- new_norms: float32 [4, 768], P(None, 'dp')
- next_mom_qkv: float32 [768, 2304], P(None, 'dp')
- next_mom_out: float32 [768, 768], P(None, 'dp')
- next_mom_fc1: float32 [768, 3072], P(None, 'dp')
- next_mom_fc2: float32 [768, 3072], P(None, 'dp')
- next_adam_mean: float32 [4, 768], P(None, 'dp')
- next_adam_var: float32 [4, 768], P(None, 'dp')
The draws below stay inside these ranges and needn't reach their ends.
All inputs are finite; a program needn't handle non-finite values.
Results may differ from the reference program's by a relative error of at most 0.024.
Values may be sent and summed in bfloat16 or wider, within the bound.
No kernel may reach another device: no remote copies, remote signals or barrier semaphores. Data moves between devices by JAX's collectives and lax.ppermute only.
A program may use at most 256 MiB of HBM per device.

```python
import math
import jax
import jax.numpy as jnp
from jax import lax

D = 768
HEADS = 12
HEAD = 64
FF = 3072
SEQ = 197
NS_ITERS = 5
IMAGES = 128


def draw_w_qkv(key, part):
    base = jax.random.normal(key, (D, 3 * D), jnp.float32) * D ** (-0.5)
    return jnp.clip(base, -5.0, 5.0)


def draw_norm_params(key, part):
    first_key, second_key = jax.random.split(jax.random.fold_in(key, 7))
    gains = jax.random.uniform(first_key, (2, D), jnp.float32, 0.5, 1.5)
    shifts = jnp.clip(jax.random.normal(second_key, (2, D), jnp.float32) * 0.3, -1.5, 1.5)
    return jnp.stack([gains[0], shifts[0], gains[1], shifts[1]])


def levels(key, shape, cuts, least, largest):
    def one(dim, parts):
        draws = jax.random.uniform(jax.random.fold_in(jax.random.fold_in(key, 6), dim), (parts,), jnp.float32, least / len(cuts), largest / len(cuts))
        return jnp.repeat(jnp.exp(draws), shape[dim] // parts).reshape((-1,) + (1,) * (len(shape) - dim - 1))

    level = one(*cuts[0])
    for cut in cuts[1:]:
        level = level * one(*cut)
    return level


def centred(rng, extent, scale, most, shards=(), dtype=jnp.bfloat16):
    values = scale * jax.random.normal(rng, extent, jnp.float32)
    if shards:
        values = values * levels(rng, extent, shards, -0.22, 0.18)
    return jnp.clip(values, -most, most).astype(dtype)


def setup_inputs(seed: int = 0) -> dict:
    key_of = jax.random.split(jax.random.key(seed), 14)
    return {
        "inputs": centred(key_of[0], (IMAGES, SEQ, D), 1.0, 6.0, ((0, 32),)),
        "out_grad": centred(key_of[1], (IMAGES, SEQ, D), 1.0, 6.0, ((0, 32),)),
        "w_qkv": draw_w_qkv(jax.random.fold_in(key_of[13], 71), 0),
        "w_out": centred(key_of[3], (D, D), (D // 8) ** -0.5, 0.625, ((1, 32),), jnp.float32),
        "w_fc1": centred(key_of[4], (D, FF), D ** -0.5, 0.21875, ((1, 32),), jnp.float32),
        "w_fc2": centred(key_of[5], (D, FF), FF ** -0.5, 0.109375, ((1, 32),), jnp.float32),
        "norm_params": draw_norm_params(jax.random.fold_in(key_of[13], 71), 0),
        "mom_qkv": centred(key_of[7], (D, 3 * D), 20.0, 128.0, ((1, 32),), jnp.float32),
        "mom_out": centred(key_of[8], (D, D), 20.0, 128.0, ((1, 32),), jnp.float32),
        "mom_fc1": centred(key_of[9], (D, FF), 20.0, 128.0, ((1, 32),), jnp.float32),
        "mom_fc2": centred(key_of[10], (D, FF), 20.0, 128.0, ((1, 32),), jnp.float32),
        "adam_mean": centred(key_of[11], (4, D), 10.0, 64.0, ((1, 32),), jnp.float32),
        "adam_var": jnp.clip(jnp.exp(math.log(50.0) - 2.3025851 * jax.random.uniform(key_of[12], (4, D), jnp.float32) ** levels(key_of[12], (4, D), ((1, 32),), -0.2, 0.2)), 5.0, 50.0),
    }


ln_eps = 1e-06
norm_eps = 1e-07
ns_first = 3.4445
ns_second = -4.775
ns_third = 2.0315
muon_rate = 0.06
decay_rate = 0.1
momentum_keep = 0.95
adam_rate = 0.1
adam_first = 0.9
adam_second = 0.999
adam_eps = 1e-08
step_count = 3.0

def rounded(values):
    return lax.optimization_barrier(values.astype(jnp.bfloat16))

def widened(values):
    return values.astype(jnp.float32)

def layer_norm(values, gain, shift):
    center = lax.optimization_barrier(jnp.mean(values, axis=-1, keepdims=True))
    centered = values - center
    inverse = lax.rsqrt(lax.optimization_barrier(jnp.mean(centered * centered, axis=-1, keepdims=True)) + ln_eps)
    normed = centered * inverse
    return (normed * gain + shift, normed, inverse)

def norm_back(grad_norm, normed, inverse, gain):
    scaled = grad_norm * gain
    return inverse * (scaled - lax.optimization_barrier(jnp.mean(scaled, axis=-1, keepdims=True)) - normed * lax.optimization_barrier(jnp.mean(scaled * normed, axis=-1, keepdims=True)))

def gelu_parts(before):
    cumulative = 0.5 * (1.0 + lax.erf(before * 0.7071067811865476))
    density = jnp.exp(-0.5 * before * before) * 0.3989422804014327
    return (before * cumulative, cumulative + before * density)

def rows_product(left_side, right_side):
    return lax.dot_general(left_side, right_side, (((0,), (0,)), ((), ())), preferred_element_type=jnp.float32)

def times_transposed(left_side, right_side):
    return lax.dot_general(left_side, right_side, (((1,), (1,)), ((), ())), preferred_element_type=jnp.float32)

def block_pass(inputs, out_grad, qkv_copy, out_copy, fc1_copy, fc2_copy, gains):
    image_count = inputs.shape[0]
    row_count = image_count * SEQ
    head_shape = (image_count, SEQ, HEADS, HEAD)
    score_scale = HEAD ** (-0.5)
    tokens = widened(inputs.reshape(row_count, D))
    first_norm, normed_one, inverse_one = layer_norm(tokens, gains[0], gains[1])
    first_bf = rounded(first_norm)
    projected = rounded(jnp.dot(first_bf, qkv_copy, preferred_element_type=jnp.float32))
    query_part = widened(projected[:, :D].reshape(head_shape))
    key_part = widened(projected[:, D:2 * D].reshape(head_shape))
    value_part = widened(projected[:, 2 * D:].reshape(head_shape))
    scores = jnp.einsum('bqhe,bkhe->bhqk', query_part, key_part) * score_scale
    highest = lax.optimization_barrier(jnp.max(scores, axis=-1, keepdims=True))
    log_total = highest + jnp.log(lax.optimization_barrier(jnp.sum(jnp.exp(scores - highest), axis=-1, keepdims=True)))
    probs = jnp.exp(scores - log_total)
    probs_bf = widened(rounded(probs))
    attended = rounded(jnp.einsum('bhqk,bkhe->bqhe', probs_bf, value_part).reshape(row_count, D))
    residual = tokens + jnp.dot(attended, out_copy, preferred_element_type=jnp.float32)
    second_norm, normed_two, inverse_two = layer_norm(residual, gains[2], gains[3])
    second_bf = rounded(second_norm)
    before = jnp.dot(second_bf, fc1_copy, preferred_element_type=jnp.float32)
    activated, slope = gelu_parts(before)
    activated_bf = rounded(activated)
    block_out = rounded(residual + times_transposed(activated_bf, fc2_copy))
    upstream = out_grad.reshape(row_count, D)
    grad_fc2 = rows_product(upstream, activated_bf)
    grad_before = rounded(jnp.dot(upstream, fc2_copy, preferred_element_type=jnp.float32) * slope)
    grad_fc1 = rows_product(second_bf, grad_before)
    grad_hidden = times_transposed(grad_before, fc1_copy)
    grad_resid = widened(upstream) + norm_back(grad_hidden, normed_two, inverse_two, gains[2])
    resid_bf = rounded(grad_resid)
    grad_out = rows_product(attended, resid_bf)
    grad_attended = widened(rounded(times_transposed(resid_bf, out_copy)).reshape(head_shape))
    grad_probs = jnp.einsum('bqhe,bkhe->bhqk', grad_attended, value_part)
    grad_value = jnp.einsum('bhqk,bqhe->bkhe', probs_bf, grad_attended)
    row_dot = lax.optimization_barrier(jnp.sum(grad_probs * probs, axis=-1, keepdims=True))
    grad_scores = widened(rounded(probs * (grad_probs - row_dot) * score_scale))
    grad_query = jnp.einsum('bhqk,bkhe->bqhe', grad_scores, key_part)
    grad_key = jnp.einsum('bhqk,bqhe->bkhe', grad_scores, query_part)
    grad_proj = rounded(jnp.concatenate([grad_query.reshape(row_count, D), grad_key.reshape(row_count, D), grad_value.reshape(row_count, D)], axis=1))
    grad_qkv = rows_product(first_bf, grad_proj)
    grad_first = times_transposed(grad_proj, qkv_copy)
    grad_tokens = grad_resid + norm_back(grad_first, normed_one, inverse_one, gains[0])
    grad_norms = jnp.stack([lax.optimization_barrier(jnp.sum(grad_first * normed_one, axis=0)), lax.optimization_barrier(jnp.sum(grad_first, axis=0)), lax.optimization_barrier(jnp.sum(grad_hidden * normed_two, axis=0)), lax.optimization_barrier(jnp.sum(grad_hidden, axis=0))])
    input_grad = grad_tokens.astype(jnp.bfloat16).reshape(inputs.shape)
    return (block_out.reshape(inputs.shape), input_grad, (grad_qkv, grad_out, grad_fc1, grad_fc2, grad_norms))

def orthogonalize(moment):
    current = moment / (jnp.sqrt(jnp.sum(moment * moment)) + norm_eps)
    for iteration in range(NS_ITERS):
        lowered = rounded(current)
        gram = rounded(times_transposed(lowered, lowered))
        first_term = jnp.dot(gram, lowered, preferred_element_type=jnp.float32)
        second_term = jnp.dot(gram, rounded(first_term), preferred_element_type=jnp.float32)
        current = ns_first * current + ns_second * first_term + ns_third * second_term
    return current

def reference(inputs, out_grad, w_qkv, w_out, w_fc1, w_fc2, norm_params, mom_qkv, mom_out, mom_fc1, mom_fc2, adam_mean, adam_var):
    copies = (rounded(w_qkv), rounded(w_out), rounded(w_fc1), rounded(w_fc2))
    gains = widened(rounded(norm_params))
    per_block = math.gcd(IMAGES, 16)
    block_count = IMAGES // per_block
    feed = (inputs.reshape(block_count, per_block, SEQ, D), out_grad.reshape(block_count, per_block, SEQ, D))
    start = (jnp.zeros((D, 3 * D), jnp.float32), jnp.zeros((D, D), jnp.float32), jnp.zeros((D, FF), jnp.float32), jnp.zeros((D, FF), jnp.float32), jnp.zeros((4, D), jnp.float32))

    def advance(carry, item):
        block_out, input_grad, grads = block_pass(item[0], item[1], copies[0], copies[1], copies[2], copies[3], gains)
        return (tuple((total + grad for total, grad in zip(carry, grads))), (block_out, input_grad))
    totals, stacked = lax.scan(advance, start, feed)
    block_out = stacked[0].reshape(IMAGES, SEQ, D)
    input_grad = stacked[1].reshape(IMAGES, SEQ, D)
    grad_qkv, grad_out, grad_fc1, grad_fc2, grad_norms = totals
    olds = (w_qkv, w_out, w_fc1, w_fc2)
    grads = (grad_qkv, grad_out, grad_fc1, grad_fc2)
    moms = (mom_qkv, mom_out, mom_fc1, mom_fc2)
    next_moms = [momentum_keep * mom + grad for mom, grad in zip(moms, grads)]
    news = []
    for weight, moment in zip(olds, next_moms):
        direction = orthogonalize(moment)
        news.append(weight * (1.0 - muon_rate * decay_rate) - muon_rate * 0.2 * math.sqrt(weight.shape[1]) * direction)
    next_adam_mean = adam_first * adam_mean + (1.0 - adam_first) * grad_norms
    next_adam_var = adam_second * adam_var + (1.0 - adam_second) * grad_norms * grad_norms
    fixed_mean = next_adam_mean / (1.0 - adam_first ** step_count)
    fixed_var = next_adam_var / (1.0 - adam_second ** step_count)
    new_norms = norm_params - adam_rate * fixed_mean / (jnp.sqrt(fixed_var) + adam_eps)
    return (block_out, input_grad, grad_qkv, grad_out, grad_fc1, grad_fc2, grad_norms, news[0], news[1], news[2], news[3], new_norms, next_moms[0], next_moms[1], next_moms[2], next_moms[3], next_adam_mean, next_adam_var)
```

```python
import functools
import math

import jax
import jax.numpy as jnp
from jax import lax
from jax.experimental import pallas as pl
from jax.experimental.pallas import tpu as pltpu
from jax.sharding import PartitionSpec as P

HEAD = 64
NS_ITERS = 5
MATRICES = 4

ln_eps = 1e-06
norm_eps = 1e-07
ns_first = 3.4445
ns_second = -4.775
ns_third = 2.0315
muon_rate = 0.06
decay_rate = 0.1
momentum_keep = 0.95
adam_rate = 0.1
adam_first = 0.9
adam_second = 0.999
adam_eps = 1e-08
step_count = 3.0

BF = jnp.bfloat16
F32 = jnp.float32


class Grid:
    def __init__(self, count):
        half = count // 2
        best = None
        for a in range(1, half + 1):
            for b in range(1, a + 1):
                if half % (a * b) == 0 and half // (a * b) <= b:
                    c = half // (a * b)
                    if best is None or a - c < best[0] - best[2]:
                        best = (a, b, c)
        self.sizes = best + (2,)
        self.count = count

    def digits(self, index):
        out = []
        for size in reversed(self.sizes):
            out.append(index % size)
            index = index // size
        return tuple(reversed(out))

    def index(self, digits):
        index = 0
        for size, digit in zip(self.sizes, digits):
            index = index * size + digit
        return index

    def swap(self, values, offset):
        pairs = []
        for source in range(self.count):
            digits = tuple(d ^ o for d, o in zip(self.digits(source), offset))
            pairs.append((source, self.index(digits)))
        return lax.ppermute(values, "dp", pairs)

    def along_z(self, values, j):
        return self.swap(values, (j, 0, 0, 0))

    def along_core(self, values):
        return self.swap(values, (0, 0, 0, 1))

    def plane_offsets(self):
        return [(jy, jx) for jy in range(self.sizes[1]) for jx in range(self.sizes[2])]

    def in_plane(self, values, jy, jx):
        return self.swap(values, (0, jy, jx, 0))


def line_blocks(grid, shard):
    return [shard] + [grid.along_z(shard, j) for j in range(1, grid.sizes[0])]


def plane_blocks(grid, own):
    if grid.sizes[1:3] == (2, 2):
        half = own.shape[0] // 2
        over_x = grid.in_plane(own, 0, 1)
        over_y = grid.in_plane(own, 1, 0)
        first = grid.in_plane(over_x[:half], 1, 0)
        second = grid.in_plane(over_y[half:], 0, 1)
        return [own, over_x, over_y, jnp.concatenate([first, second], axis=0)]
    return [own] + [grid.in_plane(own, jy, jx) for jy, jx in grid.plane_offsets()[1:]]


def plane_sum(grid, blocks):
    if grid.sizes[1:3] == (2, 2):
        half = blocks[0].shape[0] // 2
        from_x = grid.in_plane(blocks[3][:half], 0, 1)
        from_y = grid.in_plane(blocks[3][half:], 1, 0)
        to_y = jnp.concatenate([add(blocks[2][:half], from_x), blocks[2][half:]], axis=0)
        to_x = jnp.concatenate([blocks[1][:half], add(blocks[1][half:], from_y)], axis=0)
        got_x = grid.in_plane(to_x, 0, 1)
        got_y = grid.in_plane(to_y, 1, 0)
        return add(blocks[0], got_x, got_y)
    got = [
        grid.in_plane(block, jy, jx)
        for block, (jy, jx) in zip(blocks[1:], grid.plane_offsets()[1:])
    ]
    return add(blocks[0], *got)


def add(*terms):
    total = terms[0].astype(F32)
    for term in terms[1:]:
        total = total + term.astype(F32)
    return total.astype(BF)


def gather_relative(grid, shard):
    line = jnp.stack(line_blocks(grid, shard))
    plane = plane_blocks(grid, line)
    other = [grid.along_core(block) for block in plane]
    return jnp.concatenate(plane + other, axis=0)


def gather_pieces(grid, shard, place):
    z = place[0]
    line = jnp.zeros((grid.sizes[0],) + shard.shape, shard.dtype)
    for j, block in enumerate(line_blocks(grid, shard)):
        line = lax.dynamic_update_slice(line, block[None], (z ^ j, 0, 0))
    plane = plane_blocks(grid, line)
    pieces = {}
    for (jy, jx), block in zip(grid.plane_offsets(), plane):
        pieces[jy, jx, 0] = block
        pieces[jy, jx, 1] = grid.along_core(block)
    return pieces


def assemble(grid, pieces, place, rows):
    first, last = rows
    sample = pieces[0, 0, 0]
    whole = jnp.zeros(grid.sizes + (last - first, sample.shape[2]), sample.dtype)
    for (jy, jx, jc), block in pieces.items():
        at = (0, place[1] ^ jy, place[2] ^ jx, place[3] ^ jc, 0, 0)
        whole = lax.dynamic_update_slice(whole, block[:, None, None, None, first:last], at)
    return whole.reshape(grid.count * (last - first), sample.shape[2])


def z_sum(grid, blocks):
    total = blocks[0].astype(F32)
    for j in range(1, grid.sizes[0]):
        total = total + grid.along_z(blocks[j], j).astype(F32)
    return total


def scatter_relative(grid, own_half, other_half, rows):
    shape = (len(grid.plane_offsets()), grid.sizes[0], rows, own_half.shape[-1])
    arrived = grid.along_core(other_half)
    blocks = add(own_half, arrived).reshape(shape)
    line = plane_sum(grid, [blocks[a] for a in range(shape[0])])
    return z_sum(grid, [line[j] for j in range(grid.sizes[0])])


def scatter_absolute(grid, grads, place, rows):
    features = grads.shape[1]
    grads = grads.reshape(grid.sizes + (rows, features))
    half_shape = grid.sizes[:3] + (1, rows, features)
    other = lax.dynamic_slice(grads, (0, 0, 0, 1 - place[3], 0, 0), half_shape)
    mine = lax.dynamic_slice(grads, (0, 0, 0, place[3], 0, 0), half_shape)
    blocks = add(mine, grid.along_core(other))
    piece = (grid.sizes[0], 1, 1, 1, rows, features)
    parts = []
    for jy, jx in grid.plane_offsets():
        part = lax.dynamic_slice(blocks, (0, place[1] ^ jy, place[2] ^ jx, 0, 0, 0), piece)
        parts.append(part.reshape(grid.sizes[0], rows, features))
    line = plane_sum(grid, parts)
    return z_sum(
        grid,
        [
            lax.dynamic_slice(line, (place[0] ^ j, 0, 0), (1, rows, features))[0]
            for j in range(grid.sizes[0])
        ],
    )


def sum_everywhere(grid, values):
    for axis in (3, 2, 1, 0):
        total = values
        for j in range(1, grid.sizes[axis]):
            offset = tuple(j if a == axis else 0 for a in range(4))
            total = total + grid.swap(values, offset)
        values = total
    return values


def layer_norm(values, gain, shift):
    center = jnp.mean(values, axis=-1, keepdims=True)
    centered = values - center
    inverse = lax.rsqrt(jnp.mean(centered * centered, axis=-1, keepdims=True) + ln_eps)
    normed = centered * inverse
    return (normed * gain + shift, normed, inverse)


def norm_back(grad_norm, normed, inverse, gain):
    scaled = grad_norm * gain
    return inverse * (
        scaled
        - jnp.mean(scaled, axis=-1, keepdims=True)
        - normed * jnp.mean(scaled * normed, axis=-1, keepdims=True)
    )


def gelu_parts(before):
    cumulative = 0.5 * (1.0 + lax.erf(before * 0.7071067811865476))
    density = jnp.exp(-0.5 * before * before) * 0.3989422804014327
    return (before * cumulative, cumulative + before * density)


def dot_nn(left, right):
    return lax.dot_general(left, right, (((1,), (0,)), ((), ())), preferred_element_type=F32)


def dot_nt(left, right):
    return lax.dot_general(left, right, (((1,), (1,)), ((), ())), preferred_element_type=F32)


def dot_tn(left, right):
    return lax.dot_general(left, right, (((0,), (0,)), ((), ())), preferred_element_type=F32)


def forward_kernel(tokens, model, proj_ref, out_ref):
    padded = proj_ref.shape[1]
    lane = lax.broadcasted_iota(jnp.int32, (padded, 2 * HEAD), 1)
    seen = lax.broadcasted_iota(jnp.int32, (padded, padded), 1) < tokens
    scale = HEAD ** (-0.5)
    for pair in range(model // (2 * HEAD)):
        at = pair * 2 * HEAD
        query = proj_ref[0, :, at : at + 2 * HEAD]
        key = proj_ref[0, :, model + at : model + at + 2 * HEAD]
        value = proj_ref[0, :, 2 * model + at : 2 * model + at + 2 * HEAD]
        halves = []
        for part in range(2):
            mine = (lane < HEAD) if part == 0 else (lane >= HEAD)
            masked = jnp.where(mine, query, jnp.zeros_like(query))
            scores = dot_nt(masked, key) * scale
            scores = jnp.where(seen, scores, -jnp.inf)
            highest = jnp.max(scores, axis=-1, keepdims=True)
            weights = jnp.exp(scores - highest)
            total = jnp.sum(weights, axis=-1, keepdims=True)
            probs = (weights * (1.0 / total)).astype(BF)
            halves.append(dot_nn(probs, value))
        out = jnp.where(lane < HEAD, halves[0], halves[1])
        out_ref[0, :, at : at + 2 * HEAD] = out.astype(BF)


def backward_kernel(tokens, model, proj_ref, grad_ref, out_ref):
    padded = proj_ref.shape[1]
    lane = lax.broadcasted_iota(jnp.int32, (padded, 2 * HEAD), 1)
    seen = lax.broadcasted_iota(jnp.int32, (padded, padded), 0) < tokens
    scale = HEAD ** (-0.5)
    for pair in range(model // (2 * HEAD)):
        at = pair * 2 * HEAD
        query = proj_ref[0, :, at : at + 2 * HEAD]
        key = proj_ref[0, :, model + at : model + at + 2 * HEAD]
        value = proj_ref[0, :, 2 * model + at : 2 * model + at + 2 * HEAD]
        grad = grad_ref[0, :, at : at + 2 * HEAD]
        parts = []
        for part in range(2):
            mine = (lane < HEAD) if part == 0 else (lane >= HEAD)
            zero = jnp.zeros_like(query)
            scores = dot_nt(jnp.where(mine, key, zero), query) * scale
            scores = jnp.where(seen, scores, -jnp.inf)
            highest = jnp.max(scores, axis=0, keepdims=True)
            weights = jnp.exp(scores - highest)
            total = jnp.sum(weights, axis=0, keepdims=True)
            probs = weights * (1.0 / total)
            grad_probs = dot_nt(jnp.where(mine, value, zero), grad)
            row_dot = jnp.sum(grad_probs * probs, axis=0, keepdims=True)
            grad_scores = (probs * (grad_probs - row_dot) * scale).astype(BF)
            parts.append(
                (
                    dot_tn(grad_scores, key),
                    dot_nn(grad_scores, query),
                    dot_nn(probs.astype(BF), grad),
                )
            )
        for which in range(3):
            merged = jnp.where(lane < HEAD, parts[0][which], parts[1][which])
            start = which * model + at
            out_ref[0, :, start : start + 2 * HEAD] = merged.astype(BF)


def attention(projected, tokens):
    images, padded, wide = projected.shape
    model = wide // 3
    area = images * (model // HEAD) * padded * padded
    return pl.pallas_call(
        functools.partial(forward_kernel, tokens, model),
        grid=(images,),
        in_specs=[pl.BlockSpec((1, padded, wide), lambda i: (i, 0, 0))],
        out_specs=pl.BlockSpec((1, padded, model), lambda i: (i, 0, 0)),
        out_shape=jax.ShapeDtypeStruct((images, padded, model), BF),
        cost_estimate=pl.CostEstimate(
            flops=area * HEAD * 4, bytes_accessed=images * padded * wide * 3, transcendentals=area
        ),
        name="attention_forward",
    )(projected)


def attention_back(projected, grad_attended, tokens):
    images, padded, wide = projected.shape
    model = wide // 3
    area = images * (model // HEAD) * padded * padded
    return pl.pallas_call(
        functools.partial(backward_kernel, tokens, model),
        grid=(images,),
        in_specs=[
            pl.BlockSpec((1, padded, wide), lambda i: (i, 0, 0)),
            pl.BlockSpec((1, padded, model), lambda i: (i, 0, 0)),
        ],
        out_specs=pl.BlockSpec((1, padded, wide), lambda i: (i, 0, 0)),
        out_shape=jax.ShapeDtypeStruct((images, padded, wide), BF),
        cost_estimate=pl.CostEstimate(
            flops=area * HEAD * 10, bytes_accessed=images * padded * wide * 5, transcendentals=area
        ),
        name="attention_backward",
    )(projected, grad_attended)


def newton_kernel(gram_ref, own_ref, out_ref, a_ref, oa_ref, r_ref, or_ref, x_ref):
    side = gram_ref.shape[0]
    tile = 256 if side % 256 == 0 else side
    steps = side // tile
    rows = own_ref.shape[0]

    def eye(i, height):
        row = lax.broadcasted_iota(jnp.int32, (height, side), 0) + i * height
        return row == lax.broadcasted_iota(jnp.int32, (height, side), 1)

    def trace_of(ref):
        def one(i, total):
            block = ref[pl.ds(i * tile, tile), :]
            return total + jnp.sum(jnp.where(eye(i, tile), block, 0.0))

        return lax.fori_loop(0, steps, one, jnp.float32(0.0))

    size = jnp.sqrt(trace_of(gram_ref)) + norm_eps
    inverse = 1.0 / size
    x_ref[...] = own_ref[...].astype(F32) * inverse

    @pl.loop(0, steps)
    def _(i):
        at = pl.ds(i * tile, tile)
        a_ref[at, :] = gram_ref[at, :] * (inverse * inverse)

    def advance(t, alpha):
        rho = ns_second * alpha + ns_third * alpha * alpha
        tau = alpha * rho

        @pl.loop(0, steps)
        def _(i):
            at = pl.ds(i * tile, tile)
            oa_ref[at, :] = (a_ref[at, :] - jnp.where(eye(i, tile), alpha, 0.0)).astype(BF)

        @pl.loop(0, steps)
        def _(i):
            at = pl.ds(i * tile, tile)
            square = jnp.dot(oa_ref[at, :], oa_ref[...], preferred_element_type=F32)
            diagonal = jnp.where(eye(i, tile), 1.0, 0.0)
            r = (
                (ns_second + 2.0 * ns_third * alpha) * a_ref[at, :]
                - (ns_third * alpha * alpha) * diagonal
                + ns_third * square
            )
            r_ref[at, :] = r
            or_ref[at, :] = (r - rho * diagonal).astype(BF)

        x = x_ref[...]
        x_ref[...] = (ns_first + rho) * x + jnp.dot(
            x.astype(BF), or_ref[...], preferred_element_type=F32
        )

        @pl.when(t < NS_ITERS - 1)
        def _():
            @pl.loop(0, steps)
            def _(i):
                at = pl.ds(i * tile, tile)
                a = a_ref[at, :]
                r = r_ref[at, :]
                diagonal = jnp.where(eye(i, tile), 1.0, 0.0)
                t_block = (
                    alpha * r
                    + rho * (a - alpha * diagonal)
                    + jnp.dot(oa_ref[at, :], or_ref[...], preferred_element_type=F32)
                )
                rest = t_block - tau * diagonal
                u_block = (
                    tau * r
                    + rho * rest
                    + jnp.dot(rest.astype(BF), or_ref[...], preferred_element_type=F32)
                )
                a_ref[at, :] = (
                    ns_first * ns_first * a + 2.0 * ns_first * t_block + u_block
                )

        return trace_of(a_ref) / side

    lax.fori_loop(0, NS_ITERS, advance, trace_of(a_ref) / side)
    out_ref[...] = x_ref[...].astype(BF)


def newton(gram, own):
    side = gram.shape[0]
    rows = own.shape[0]
    vmem = pl.BlockSpec(memory_space=pltpu.VMEM)
    return pl.pallas_call(
        newton_kernel,
        in_specs=[vmem, vmem],
        out_specs=vmem,
        out_shape=jax.ShapeDtypeStruct((rows, side), BF),
        scratch_shapes=[
            pltpu.VMEM((side, side), F32),
            pltpu.VMEM((side, side), BF),
            pltpu.VMEM((side, side), F32),
            pltpu.VMEM((side, side), BF),
            pltpu.VMEM((rows, side), F32),
        ],
        cost_estimate=pl.CostEstimate(
            flops=2 * side * side * (13 * side + 5 * rows),
            bytes_accessed=4 * side * side + 4 * rows * side,
            transcendentals=0,
        ),
        name="newton_schulz",
    )(gram, own)


def body(
    inputs,
    out_grad,
    w_qkv,
    w_out,
    w_fc1,
    w_fc2,
    norm_params,
    mom_qkv,
    mom_out,
    mom_fc1,
    mom_fc2,
    adam_mean,
    adam_var,
):
    count = lax.axis_size("dp")
    grid = Grid(count)
    me = lax.axis_index("dp")
    place = grid.digits(me)
    images, seq, model = inputs.shape
    padded = -(-seq // 8) * 8
    rows = images * padded
    weights = (w_qkv, w_out, w_fc1, w_fc2)
    shard_rows = tuple(weight.shape[1] for weight in weights)
    qkv_rows, out_rows, fc1_rows, fc2_rows = shard_rows
    norm_cols = norm_params.shape[1]

    extra = -(-(qkv_rows + 1) // 8) * 8 - qkv_rows
    norm_row = jnp.pad(
        norm_params.astype(BF).reshape(1, 4 * norm_cols),
        ((0, extra - 1), (0, model - 4 * norm_cols)),
    )
    qkv_shard = jnp.concatenate([w_qkv.astype(BF).T, norm_row], axis=0)
    out_shard = w_out.astype(BF).T
    fc1_shard = w_fc1.astype(BF).T
    fc2_shard = w_fc2.astype(BF).T

    qkv_pieces = gather_pieces(grid, qkv_shard, place)
    qkv_t = assemble(grid, qkv_pieces, place, (0, qkv_rows))
    norm_whole = assemble(grid, qkv_pieces, place, (qkv_rows, qkv_rows + 1))
    gains = (
        norm_whole[:, : 4 * norm_cols]
        .reshape(count, 4, norm_cols)
        .transpose(1, 0, 2)
        .reshape(4, model)
        .astype(F32)
    )
    out_t = assemble(grid, gather_pieces(grid, out_shard, place), place, (0, out_rows))
    fc1_t = gather_relative(grid, fc1_shard).reshape(count * fc1_rows, model)
    fc2_t = gather_relative(grid, fc2_shard).reshape(count * fc2_rows, model)

    def widen(values):
        return jnp.pad(values, ((0, 0), (0, padded - seq), (0, 0))).reshape(rows, model)

    def narrow(values):
        return values.reshape(images, padded, model)[:, :seq].astype(BF)

    tokens = widen(inputs).astype(F32)
    first_norm, normed_one, inverse_one = layer_norm(tokens, gains[0], gains[1])
    first_bf = first_norm.astype(BF)
    projected = dot_nt(first_bf, qkv_t).astype(BF).reshape(images, padded, 3 * model)
    attended = attention(projected, seq).reshape(rows, model)
    residual = tokens + dot_nt(attended, out_t)
    second_norm, normed_two, inverse_two = layer_norm(residual, gains[2], gains[3])
    second_bf = second_norm.astype(BF)
    before = dot_nt(second_bf, fc1_t)
    activated, slope = gelu_parts(before)
    activated_bf = activated.astype(BF)
    block_out = narrow(residual + dot_nn(activated_bf, fc2_t))

    upstream = widen(out_grad)
    half = count * fc1_rows // 2

    def split_grads(hidden, features):
        other = dot_tn(hidden[:, half:], features).astype(BF)
        own = dot_tn(hidden[:, :half], features).astype(BF)
        return own, other

    own_fc2 = scatter_relative(grid, *split_grads(activated_bf, upstream), fc2_rows)
    grad_before = (dot_nt(upstream, fc2_t) * slope).astype(BF)
    own_fc1 = scatter_relative(grid, *split_grads(grad_before, second_bf), fc1_rows)
    grad_hidden = dot_nn(grad_before, fc1_t)
    grad_resid = upstream.astype(F32) + norm_back(grad_hidden, normed_two, inverse_two, gains[2])
    resid_bf = grad_resid.astype(BF)
    own_out = scatter_absolute(grid, dot_tn(resid_bf, attended).astype(BF), place, out_rows)
    grad_attended = dot_nn(resid_bf, out_t).astype(BF).reshape(images, padded, model)
    grad_proj = attention_back(projected, grad_attended, seq).reshape(rows, 3 * model)
    own_qkv = scatter_absolute(grid, dot_tn(grad_proj, first_bf).astype(BF), place, qkv_rows)
    grad_first = dot_nn(grad_proj, qkv_t)
    grad_tokens = grad_resid + norm_back(grad_first, normed_one, inverse_one, gains[0])
    input_grad = narrow(grad_tokens)
    norm_grads = jnp.stack(
        [
            jnp.sum(grad_first * normed_one, axis=0),
            jnp.sum(grad_first, axis=0),
            jnp.sum(grad_hidden * normed_two, axis=0),
            jnp.sum(grad_hidden, axis=0),
        ]
    )
    own_norm = lax.dynamic_slice(
        sum_everywhere(grid, norm_grads), (0, me * norm_cols), (4, norm_cols)
    )

    grads = [own.T for own in (own_qkv, own_out, own_fc1, own_fc2)]
    moms = (mom_qkv, mom_out, mom_fc1, mom_fc2)
    moments = [momentum_keep * mom + grad for mom, grad in zip(moms, grads)]

    assert grid.sizes[0] == MATRICES
    z = place[0]
    height = max(shard_rows)
    stacked = jnp.stack(
        [
            jnp.pad(moment.astype(BF).T, ((0, height - moment.shape[1]), (0, 0)))
            for moment in moments
        ]
    )

    def for_group(values, j):
        return lax.dynamic_slice(values, (z ^ j, 0, 0), (1,) + values.shape[1:])[0]

    own_rows = jnp.concatenate(
        [for_group(stacked, 0)]
        + [grid.along_z(for_group(stacked, j), j) for j in range(1, MATRICES)],
        axis=0,
    )
    plane = plane_blocks(grid, own_rows)
    everything = jnp.concatenate(plane + [grid.along_core(block) for block in plane], axis=0)
    gram = dot_tn(everything, everything)
    finished = newton(gram, own_rows).reshape(MATRICES, height, model)
    returned = jnp.stack(
        [finished[0]] + [grid.along_z(finished[j], j) for j in range(1, MATRICES)]
    )
    news = []
    for position, weight in enumerate(weights):
        current = for_group(returned, position)
        current = current[: shard_rows[position]].T.astype(F32)
        news.append(
            weight * (1.0 - muon_rate * decay_rate)
            - muon_rate * 0.2 * math.sqrt(count * shard_rows[position]) * current
        )
    next_adam_mean = adam_first * adam_mean + (1.0 - adam_first) * own_norm
    next_adam_var = adam_second * adam_var + (1.0 - adam_second) * own_norm * own_norm
    fixed_mean = next_adam_mean / (1.0 - adam_first**step_count)
    fixed_var = next_adam_var / (1.0 - adam_second**step_count)
    new_norms = norm_params - adam_rate * fixed_mean / (jnp.sqrt(fixed_var) + adam_eps)
    return (
        block_out,
        input_grad,
        *grads,
        own_norm,
        *news,
        new_norms,
        *moments,
        next_adam_mean,
        next_adam_var,
    )


def solution(mesh):
    batch = P("dp", None, None)
    columns = P(None, "dp")
    return jax.shard_map(
        body,
        mesh=mesh,
        in_specs=(batch,) * 2 + (columns,) * 11,
        out_specs=(batch,) * 2 + (columns,) * 16,
        check_vma=False,
    )
```
